32 devices in a mesh: ctx: 4 (over y, x), fsdp: 8 (over z, core).
Axes of the slice: x: 2, y: 2, z: 4, core: 2. Of those that a mesh axis runs over, the one named last changes fastest.
Arguments:
- tokens: bfloat16 [8, 1024, 1024], P('fsdp', 'ctx'), may hold values from -6 to 6
- positions: int32 [8, 1024], P('fsdp', 'ctx'), may hold values from 0 to 511, as said below
- block_pairs: int32 [4], replicated, may hold values from 0 to 3, as said below
- input_gain: bfloat16 [1024], P('fsdp'), may hold values from 0.5 to 1.5
- query_gain: bfloat16 [64], P('fsdp'), may hold values from 0.5 to 1.5
- key_gain: bfloat16 [64], P('fsdp'), may hold values from 0.5 to 1.5
- query_weight: bfloat16 [1024, 1024], P('fsdp'), may hold values from -0.1875 to 0.1875
- key_weight: bfloat16 [1024, 512], P('fsdp'), may hold values from -0.1875 to 0.1875
- value_weight: bfloat16 [1024, 512], P('fsdp'), may hold values from -0.1875 to 0.1875
- out_weight: bfloat16 [1024, 1024], P('fsdp'), may hold values from -2 to 2
- middle_gain: bfloat16 [1024], P('fsdp'), may hold values from 0.5 to 1.5
- gate_weight: bfloat16 [1024, 4608], P('fsdp'), may hold values from -0.1875 to 0.1875
- up_weight: bfloat16 [1024, 4608], P('fsdp'), may hold values from -0.1875 to 0.1875
- down_weight: bfloat16 [4608, 1024], P('fsdp'), may hold values from -0.09375 to 0.09375
- cotangent: bfloat16 [8, 1024, 1024], P('fsdp', 'ctx'), may hold values from -6 to 6
Outputs:
- layer_out: bfloat16 [8, 1024, 1024], P('fsdp', 'ctx')
- grad_tokens: bfloat16 [8, 1024, 1024], P('fsdp', 'ctx')
- grad_input_gain: float32 [1024], P('fsdp')
- grad_query_gain: float32 [64], P('fsdp')
- grad_key_gain: float32 [64], P('fsdp')
- grad_query_weight: float32 [1024, 1024], P('fsdp')
- grad_key_weight: float32 [1024, 512], P('fsdp')
- grad_value_weight: float32 [1024, 512], P('fsdp')
- grad_out_weight: float32 [1024, 1024], P('fsdp')
- grad_middle_gain: float32 [1024], P('fsdp')
- grad_gate_weight: float32 [1024, 4608], P('fsdp')
- grad_up_weight: float32 [1024, 4608], P('fsdp')
- grad_down_weight: float32 [4608, 1024], P('fsdp')
The draws below stay inside these ranges and needn't reach their ends.
Inputs may be any that keep to these rules, and one draw needn't show every extreme that they name: A permutation; in every sequence, index c of ctx holds the blocks of 128 tokens numbered block_pairs[c] and 7 - block_pairs[c] in true order, in that order. `positions`: each row's place within its document, documents following one another in true order; the first document of a sequence covers its first 512 tokens in true order, and a document starts at true place 1024 // 2.
All inputs are finite; a program needn't handle non-finite values.
Results may differ from the reference program's by a relative error of at most 0.025.
Values may be sent and summed in bfloat16 or wider, within the bound.
No kernel may reach another device: no remote copies, remote signals or barrier semaphores. Data moves between devices by JAX's collectives and lax.ppermute only.
A program may use at most 192 MiB of HBM per device.

```python
import jax
import jax.numpy as jnp
from jax import lax

D = 1024
H = 16
HD = 64
KV = 8
FF = 4608
SEQ_LEN = 1024
SEQS = 8
N_CTX = 4


def stored_order(key):
    return jax.random.permutation(jax.random.fold_in(key, 11), N_CTX).astype(jnp.int32)


def draw_block_pairs(key, part):
    return stored_order(key)


def draw_positions(key, part):
    order_perm = stored_order(key)
    rows_each = SEQ_LEN // N_CTX
    half_rows = rows_each // 2
    half_seq = SEQ_LEN // 2
    row_ids = jnp.arange(SEQ_LEN, dtype=jnp.int32)
    owner = row_ids // rows_each
    within = row_ids % rows_each
    picked = jnp.take(order_perm, owner)
    blocks_of = jnp.where(within < half_rows, picked, 2 * N_CTX - 1 - picked)
    places = (blocks_of * half_rows + within % half_rows).astype(jnp.int32)
    random_starts = jax.random.randint(jax.random.fold_in(key, 12), (SEQS, SEQ_LEN), 0, max(SEQ_LEN // 4, 2)) == 0
    true_ids = jnp.broadcast_to(row_ids[None, :], (SEQS, SEQ_LEN))
    starts = jnp.logical_and(random_starts, true_ids > half_seq)
    starts = jnp.logical_or(starts, true_ids == 0)
    starts = jnp.logical_or(starts, true_ids == half_seq)
    latest = lax.cummax(jnp.where(starts, true_ids, 0), axis=1)
    within_doc = true_ids - latest
    return jnp.take(within_doc, places, axis=1).astype(jnp.int32)


def shard_levels(stream_key, dims, shards, least, largest):
    def one(dim, shards_of):
        steps = jax.random.uniform(jax.random.fold_in(jax.random.fold_in(stream_key, 6), dim), (shards_of,), jnp.float32, least / len(shards), largest / len(shards))
        return jnp.repeat(jnp.exp(steps), dims[dim] // shards_of).reshape((-1,) + (1,) * (len(dims) - dim - 1))

    level = one(*shards[0])
    for cut in shards[1:]:
        level = level * one(*cut)
    return level


def bell_draw(key, dims, width, most, cuts=(), held_as=jnp.bfloat16):
    entries = jax.random.normal(key, dims, jnp.float32) * width
    if len(cuts) > 0:
        entries = shard_levels(key, dims, cuts, -0.22, 0.18) * entries
    return jnp.clip(entries, min=-most, max=most).astype(held_as)


def setup_inputs(seed: int = 0) -> dict:
    key_of = jax.random.split(jax.random.key(seed), 16)
    tokens = bell_draw(key_of[0], (SEQS, SEQ_LEN, D), 1.0, 6.0, ((0, 8), (1, 4)))
    positions = draw_positions(jax.random.fold_in(key_of[15], 71), 0)
    block_pairs = draw_block_pairs(jax.random.fold_in(key_of[15], 71), 0)
    input_gain = jnp.clip(1.0 + 0.1 * jax.random.normal(key_of[3], (D,), jnp.float32), 0.5, 1.5).astype(jnp.bfloat16)
    query_gain = jnp.clip(1.0 + 0.1 * jax.random.normal(key_of[4], (HD,), jnp.float32), 0.5, 1.5).astype(jnp.bfloat16)
    key_gain = jnp.clip(1.0 + 0.1 * jax.random.normal(key_of[5], (HD,), jnp.float32), 0.5, 1.5).astype(jnp.bfloat16)
    query_weight = bell_draw(key_of[6], (D, H * HD), D ** -0.5, 0.1875, ((0, 8),))
    key_weight = bell_draw(key_of[7], (D, KV * HD), D ** -0.5, 0.1875, ((0, 8),))
    value_weight = bell_draw(key_of[8], (D, KV * HD), D ** -0.5, 0.1875, ((0, 8),))
    out_weight = bell_draw(key_of[9], (H * HD, D), (max(1, H * HD * 8 // SEQ_LEN)) ** -0.5, 2.0, ((0, 8),))
    middle_gain = jnp.clip(1.0 + 0.1 * jax.random.normal(key_of[10], (D,), jnp.float32), 0.5, 1.5).astype(jnp.bfloat16)
    gate_weight = bell_draw(key_of[11], (D, FF), D ** -0.5, 0.1875, ((0, 8),))
    up_weight = bell_draw(key_of[12], (D, FF), D ** -0.5, 0.1875, ((0, 8),))
    down_weight = bell_draw(key_of[13], (FF, D), FF ** -0.5, 0.09375, ((0, 8),))
    cotangent = bell_draw(key_of[14], (SEQS, SEQ_LEN, D), 1.0, 6.0, ((0, 8), (1, 4)))
    return dict(tokens=tokens, positions=positions, block_pairs=block_pairs, input_gain=input_gain, query_gain=query_gain, key_gain=key_gain, query_weight=query_weight, key_weight=key_weight, value_weight=value_weight, out_weight=out_weight, middle_gain=middle_gain, gate_weight=gate_weight, up_weight=up_weight, down_weight=down_weight, cotangent=cotangent)


epsilon = 1e-05
theta_base = 1000000.0
score_scale = 0.125
masked_value = -1e+30

@jax.custom_vjp
def low(v):
    return lax.optimization_barrier(v.astype(jnp.bfloat16)).astype(jnp.float32)

@jax.custom_vjp
def low_back(v):
    return v

def low_keep(v):
    return (low(v), None)

def low_pass(kept, grad):
    return (grad,)

def back_keep(v):
    return (v, None)

def back_low(kept, grad):
    return (low(grad),)
low.defvjp(low_keep, low_pass)
low_back.defvjp(back_keep, back_low)

def matmul(left, right):
    return jnp.dot(left, right, precision=lax.Precision.HIGHEST)

def root_norm(values, scale_vec):
    return values * lax.rsqrt(lax.optimization_barrier(jnp.mean(values * values, axis=-1, keepdims=True)) + epsilon) * scale_vec

def rotate(values, places):
    half_dim = HD // 2
    freqs = theta_base ** (-(jnp.arange(half_dim, dtype=jnp.float32) * 2.0) / HD)
    angles = places.astype(jnp.float32)[:, None] * freqs[None, :]
    cosine = jnp.cos(angles)[:, None, :]
    sine = jnp.sin(angles)[:, None, :]
    first_half = values[..., :half_dim]
    second_half = values[..., half_dim:]
    return jnp.concatenate([first_half * cosine - second_half * sine, second_half * cosine + first_half * sine], axis=-1)

def true_places(block_pairs, rank_count, rows_each):
    half_rows = rows_each // 2
    row_ids = jnp.arange(rank_count * rows_each, dtype=jnp.int32)
    owner = row_ids // rows_each
    within = row_ids % rows_each
    ranks_row = jnp.arange(rank_count, dtype=jnp.int32)
    picked = lax.optimization_barrier(jnp.sum(jnp.where(owner[:, None] == ranks_row[None, :], block_pairs[None, :], 0), axis=1)).astype(jnp.int32)
    blocks_of = jnp.where(within < half_rows, picked, 2 * rank_count - 1 - picked)
    return (blocks_of * half_rows + within % half_rows).astype(jnp.int32)

def sequence_layer(hidden, places, order, input_gain, query_gain, key_gain, query_weight, key_weight, value_weight, out_weight, middle_gain, gate_weight, up_weight, down_weight):
    length = hidden.shape[0]
    groups = H // KV
    normed = low(root_norm(hidden, input_gain))
    query_proj = low_back(matmul(normed, query_weight)).reshape(length, H, HD)
    key_proj = low_back(matmul(normed, key_weight)).reshape(length, KV, HD)
    value_proj = low_back(low(matmul(normed, value_weight))).reshape(length, KV, HD)
    query_rot = low(rotate(root_norm(query_proj, query_gain), places)).reshape(length, KV, groups, HD)
    key_rot = low(rotate(root_norm(key_proj, key_gain), places))
    scores = jnp.einsum('qgrd,kgd->grqk', query_rot, key_rot, precision=lax.Precision.HIGHEST) * score_scale
    scores = low_back(scores)
    allowed = order[:, None] >= order[None, :]
    scores = jnp.where(allowed[None, None], scores, masked_value)
    probs = low(jax.nn.softmax(scores, axis=-1))
    mixed = jnp.einsum('grqk,kgd->qgrd', probs, value_proj, precision=lax.Precision.HIGHEST).reshape(length, H * HD)
    mixed = low_back(low(mixed))
    middle = hidden + low_back(matmul(mixed, out_weight))
    normed_two = low(root_norm(middle, middle_gain))
    gate = low_back(matmul(normed_two, gate_weight))
    up_values = low_back(matmul(normed_two, up_weight))
    activated = low(jax.nn.silu(gate) * up_values)
    return middle + matmul(activated, down_weight)

def reference(tokens, positions, block_pairs, input_gain, query_gain, key_gain, query_weight, key_weight, value_weight, out_weight, middle_gain, gate_weight, up_weight, down_weight, cotangent):
    order = true_places(block_pairs, N_CTX, SEQ_LEN // N_CTX)
    weights = tuple((item.astype(jnp.float32) for item in (input_gain, query_gain, key_gain, query_weight, key_weight, value_weight, out_weight, middle_gain, gate_weight, up_weight, down_weight)))

    def whole(hidden_all, *params):

        def single(item):
            return sequence_layer(item[0], item[1], order, *params)
        return lax.map(jax.checkpoint(single), (hidden_all, positions))
    result, pull = jax.vjp(whole, tokens.astype(jnp.float32), *weights)
    grads = pull(cotangent.astype(jnp.float32))
    return (result.astype(jnp.bfloat16), grads[0].astype(jnp.bfloat16), grads[1], grads[2], grads[3], grads[4], grads[5], grads[6], grads[7], grads[8], grads[9], grads[10], grads[11])
```

```python
import functools

import jax
import jax.numpy as jnp
from jax import lax
from jax.experimental import pallas as pl
from jax.experimental.pallas import tpu as pltpu
from jax.sharding import PartitionSpec as P


H = 16
HD = 64
KV = 8
GROUPS = H // KV

epsilon = 1e-05
theta_base = 1000000.0
score_scale = 0.125
masked_value = -1e30


def dot_plain(left, right):
    return jnp.dot(left, right, preferred_element_type=jnp.float32)


def times_transposed(left, right):
    return lax.dot_general(
        left, right, (((1,), (1,)), ((), ())), preferred_element_type=jnp.float32
    )


def transposed_times(left, right):
    return lax.dot_general(
        left, right, (((0,), (0,)), ((), ())), preferred_element_type=jnp.float32
    )


def exact_dot(left, right):
    return jnp.dot(
        left, right, preferred_element_type=jnp.float32, precision=lax.Precision.HIGHEST
    )


def unit_norm(values):
    inverse = lax.rsqrt(jnp.mean(values * values, axis=-1, keepdims=True) + epsilon)
    return values * inverse, inverse


def norm_backward(scaled, normal, inverse):
    inner = jnp.mean(scaled * normal, axis=-1, keepdims=True)
    return inverse * (scaled - normal * inner)


def lane_tables(width):
    row = lax.broadcasted_iota(jnp.int32, (width, width), 0)
    col = lax.broadcasted_iota(jnp.int32, (width, width), 1)
    mean = jnp.where(row // HD == col // HD, 1.0 / HD, 0.0).astype(jnp.float32)
    low = col % HD < HD // 2
    partner = jnp.where(low, col + HD // 2, col - HD // 2)
    swap = jnp.where(row == partner, 1.0, 0.0).astype(jnp.float32)
    lane = lax.broadcasted_iota(jnp.int32, (1, width), 1)
    sign = jnp.where(lane % HD < HD // 2, -1.0, 1.0).astype(jnp.float32)
    return mean, swap, sign


def chunk_widths(width):
    step = min(width, 2 * HD)
    return [(start, step) for start in range(0, width, step)]


def attention_forward_kernel(
    qkv_ref, cos_ref, sin_ref, gq_ref, gk_ref, ob_ref, qs_ref, ks_ref, vs_ref, os_ref,
    *, q_width, kv_width, rows, block
):
    q_heads = q_width // HD
    kv_heads = kv_width // HD
    for base, width, gain_ref, out_ref, scale in (
        (0, q_width, gq_ref, qs_ref, score_scale),
        (q_width, kv_width, gk_ref, ks_ref, 1.0),
    ):
        for start, step in chunk_widths(width):
            mean, swap, sign = lane_tables(step)
            for row in range(0, rows, block):
                here = pl.ds(row, block)
                raw = qkv_ref[here, pl.ds(base + start, step)]
                inverse = lax.rsqrt(exact_dot(raw * raw, mean) + epsilon)
                normed = raw * inverse * gain_ref[:, :step]
                turned = normed * cos_ref[here, :step] + exact_dot(normed, swap) * (
                    sin_ref[here, :step] * sign
                )
                low = turned.astype(jnp.bfloat16) * jnp.bfloat16(scale)
                for part in range(step // HD):
                    out_ref[start // HD + part, here, :] = low[:, part * HD : (part + 1) * HD]
    for head in range(kv_heads):
        at = q_width + kv_width + head * HD
        vs_ref[head] = qkv_ref[:, pl.ds(at, HD)].astype(jnp.bfloat16)

    def one_head(head, carry):
        pair = head // GROUPS
        for row in range(0, rows, block):
            upto = row + block
            q_here = qs_ref[head, pl.ds(row, block), :]
            scores = times_transposed(q_here, ks_ref[pair, pl.ds(0, upto), :])
            own = lax.broadcasted_iota(jnp.int32, (block, upto), 0) + row
            other = lax.broadcasted_iota(jnp.int32, (block, upto), 1)
            scores = jnp.where(own >= other, scores, masked_value)
            top = jnp.max(scores, axis=-1, keepdims=True)
            expo = jnp.exp(scores - top)
            probs = (expo * (1.0 / jnp.sum(expo, axis=-1, keepdims=True))).astype(jnp.bfloat16)
            mixed = dot_plain(probs, vs_ref[pair, pl.ds(0, upto), :])
            os_ref[head, pl.ds(row, block), :] = mixed.astype(jnp.bfloat16)
        return carry

    lax.fori_loop(0, q_heads, one_head, 0)
    for head in range(q_heads):
        ob_ref[:, head * HD : (head + 1) * HD] = os_ref[head]


def attention_backward_kernel(
    qkv_ref, cos_ref, sin_ref, gq_ref, gk_ref, qs_ref, ks_ref, vs_ref, dob_ref,
    dqkv_ref, gains_ref, do_ref, dq_ref, dk_ref, dv_ref,
    *, q_width, kv_width, rows, block
):
    q_heads = q_width // HD
    kv_heads = kv_width // HD
    for head in range(q_heads):
        do_ref[head] = dob_ref[:, head * HD : (head + 1) * HD]
    dk_ref[...] = jnp.zeros_like(dk_ref)
    dv_ref[...] = jnp.zeros_like(dv_ref)

    def one_head(head, carry):
        pair = head // GROUPS
        for row in range(0, rows, block):
            upto = row + block
            here = pl.ds(row, block)
            seen = pl.ds(0, upto)
            q_here = qs_ref[head, here, :]
            do_here = do_ref[head, here, :]
            scores = times_transposed(q_here, ks_ref[pair, seen, :])
            own = lax.broadcasted_iota(jnp.int32, (block, upto), 0) + row
            other = lax.broadcasted_iota(jnp.int32, (block, upto), 1)
            scores = jnp.where(own >= other, scores, masked_value)
            top = jnp.max(scores, axis=-1, keepdims=True)
            expo = jnp.exp(scores - top)
            probs = expo * (1.0 / jnp.sum(expo, axis=-1, keepdims=True))
            prob_grad = times_transposed(do_here, vs_ref[pair, seen, :])
            inner = jnp.sum(probs * prob_grad, axis=-1, keepdims=True)
            score_grad = (probs * (prob_grad - inner)).astype(jnp.bfloat16)
            dq_ref[head, here, :] = dot_plain(score_grad, ks_ref[pair, seen, :]) * score_scale
            dk_ref[pair, seen, :] += transposed_times(score_grad, q_here)
            dv_ref[pair, seen, :] += transposed_times(probs.astype(jnp.bfloat16), do_here)
        return carry

    lax.fori_loop(0, q_heads, one_head, 0)
    gains_ref[...] = jnp.zeros_like(gains_ref)
    for slot, base, width, gain_ref, grad_ref in (
        (0, 0, q_width, gq_ref, dq_ref),
        (1, q_width, kv_width, gk_ref, dk_ref),
    ):
        for start, step in chunk_widths(width):
            mean, swap, sign = lane_tables(step)
            for row in range(0, rows, block):
                here = pl.ds(row, block)
                first = start // HD
                turned = jnp.concatenate(
                    [grad_ref[first + part, here, :] for part in range(step // HD)], axis=1
                )
                normed_grad = turned * cos_ref[here, :step] - exact_dot(turned, swap) * (
                    sin_ref[here, :step] * sign
                )
                raw = qkv_ref[here, pl.ds(base + start, step)]
                inverse = lax.rsqrt(exact_dot(raw * raw, mean) + epsilon)
                unit = raw * inverse
                gains_ref[slot : slot + 1, :step] += jnp.sum(
                    normed_grad * unit, axis=0, keepdims=True
                )
                scaled = normed_grad * gain_ref[:, :step]
                raw_grad = inverse * (scaled - unit * exact_dot(scaled * unit, mean))
                dqkv_ref[here, pl.ds(base + start, step)] = raw_grad.astype(jnp.bfloat16)
    for head in range(kv_heads):
        at = q_width + kv_width + head * HD
        dqkv_ref[:, at : at + HD] = dv_ref[head].astype(jnp.bfloat16)


def spread_kernel(parts_ref, gate_ref, up_ref, *, shards_of, ranks, piece):
    half = shards_of * piece
    for base, out_ref in ((0, gate_ref), (half, up_ref)):
        out_ref[...] = jnp.concatenate(
            [
                parts_ref[rank, :, base + shard * piece : base + (shard + 1) * piece]
                for shard in range(shards_of)
                for rank in range(ranks)
            ],
            axis=1,
        ).astype(jnp.float32)


def pick_kernel(rank_ref, gate_ref, up_ref, out_ref, *, shards_of, ranks, piece):
    half = shards_of * piece
    for rank in range(ranks):

        @pl.when(rank_ref[0] == rank)
        def _():
            for base, in_ref in ((0, gate_ref), (half, up_ref)):
                out_ref[:, base : base + half] = jnp.concatenate(
                    [
                        in_ref[:, (shard * ranks + rank) * piece : (shard * ranks + rank + 1) * piece]
                        for shard in range(shards_of)
                    ],
                    axis=1,
                )


def call_kernel(kernel, out_shapes, scratch=(), smem_first=False, count=0):
    vmem = pl.BlockSpec(memory_space=pltpu.VMEM)
    in_specs = [vmem] * count
    if smem_first:
        in_specs[0] = pl.BlockSpec(memory_space=pltpu.SMEM)
    return pl.pallas_call(
        kernel,
        out_shape=out_shapes,
        in_specs=in_specs,
        out_specs=jax.tree.map(lambda _: vmem, out_shapes),
        scratch_shapes=scratch,
        compiler_params=pltpu.CompilerParams(vmem_limit_bytes=56 * 1024 * 1024),
    )


def shards(
    tokens,
    positions,
    block_pairs,
    input_gain,
    query_gain,
    key_gain,
    query_weight,
    key_weight,
    value_weight,
    out_weight,
    middle_gain,
    gate_weight,
    up_weight,
    down_weight,
    cotangent,
):
    ranks = lax.axis_size("ctx")
    owners = lax.axis_size("fsdp")
    me = lax.axis_index("ctx")
    own_tokens = tokens[0]
    rows_here, model = own_tokens.shape
    half_rows = rows_here // 2
    rows = rows_here * ranks
    others = range(1, ranks)
    bf16 = jnp.bfloat16
    f32 = jnp.float32
    q_width = H // ranks * HD
    kv_width = KV // ranks * HD
    width = q_width + 2 * kv_width
    model_part = model // owners
    hidden_width = gate_weight.shape[1]
    piece = hidden_width // (owners * ranks)
    hidden_here = owners * piece

    def send(value, step):
        return lax.ppermute(value, "ctx", [(i, i ^ step) for i in range(ranks)])

    def gather_ctx(value):
        return [value] + [send(value, step) for step in others]

    def by_rank(parts):
        stack = jnp.zeros((ranks,) + parts[0].shape, parts[0].dtype)
        for step, part in enumerate(parts):
            stack = lax.dynamic_update_index_in_dim(stack, part, me ^ step, 0)
        return stack

    place = lax.axis_index("fsdp")
    core = place % 2
    chip = place // 2
    chips = owners // 2

    def send_owner(value, step):
        return lax.ppermute(value, "fsdp", [(i, i ^ step) for i in range(owners)])

    def gather_owners(value):
        stack = jnp.zeros((chips,) + value.shape, value.dtype)
        for step in range(chips):
            part = send_owner(value, 2 * step) if step else value
            stack = lax.dynamic_update_index_in_dim(stack, part, chip ^ step, 0)
        partner = send_owner(stack, 1)
        first = jnp.where(core == 0, stack, partner)
        second = jnp.where(core == 0, partner, stack)
        return jnp.stack([first, second], axis=1)

    def scatter_owners(value):
        mine = jnp.where(core == 0, value[:, 0], value[:, 1])
        theirs = send_owner(jnp.where(core == 0, value[:, 1], value[:, 0]), 1)
        pair = (mine.astype(f32) + theirs.astype(f32)).astype(bf16)
        total = lax.dynamic_index_in_dim(pair, chip, 0, keepdims=False).astype(f32)
        for step in range(1, chips):
            entry = lax.dynamic_index_in_dim(pair, chip ^ step, 0, keepdims=False)
            total = total + send_owner(entry, 2 * step).astype(f32)
        return total.astype(bf16)

    hold = lax.optimization_barrier

    def block_starts(step):
        low = lax.dynamic_index_in_dim(block_pairs, me ^ step, 0, keepdims=False)
        return low * half_rows, (2 * ranks - 1 - low) * half_rows

    def true_order(parts):
        out = jnp.zeros((rows,) + parts[0].shape[1:], parts[0].dtype)
        for step, part in enumerate(parts):
            low, high = block_starts(step)
            out = lax.dynamic_update_slice_in_dim(out, part[:half_rows], low, 0)
            out = lax.dynamic_update_slice_in_dim(out, part[half_rows:], high, 0)
        return out

    def rows_of(value, step):
        low, high = block_starts(step)
        return jnp.concatenate(
            [
                lax.dynamic_slice_in_dim(value, low, half_rows, 0),
                lax.dynamic_slice_in_dim(value, high, half_rows, 0),
            ],
            axis=0,
        )

    def columns(weight, size):
        return lax.dynamic_slice_in_dim(weight, me * size, size, 1)

    def gain_row(gain):
        return jnp.pad(gain, (0, width - gain.shape[0]))[None]

    attn_pack = jnp.concatenate(
        [
            columns(query_weight, q_width),
            columns(key_weight, kv_width),
            columns(value_weight, kv_width),
        ],
        axis=1,
    )
    gain_pack = jnp.concatenate(
        [gain_row(g) for g in (input_gain, middle_gain, query_gain, key_gain)]
        + [jnp.zeros((12, width), bf16)],
        axis=0,
    )
    token_parts = gather_ctx(own_tokens)
    place_parts = gather_ctx(positions[0])
    attn_all = gather_owners(
        jnp.concatenate([attn_pack, gain_pack], axis=0)
    ).reshape(owners, model_part + 16, width)
    qkv_weight = attn_all[:, :model_part].reshape(model, width)
    gain_one = attn_all[:, model_part, :model_part].reshape(1, model).astype(f32)
    gain_two = attn_all[:, model_part + 1, :model_part].reshape(1, model).astype(f32)
    head_part = HD // owners
    gain_query = attn_all[:, model_part + 2, :head_part].reshape(1, HD).astype(f32)
    gain_key = attn_all[:, model_part + 3, :head_part].reshape(1, HD).astype(f32)
    gain_query = jnp.tile(gain_query, (1, 2))
    gain_key = jnp.tile(gain_key, (1, 2))
    out_full = lax.all_gather(out_weight, "fsdp", axis=0, tiled=True)
    pick = functools.partial(pick_kernel, shards_of=owners, ranks=ranks, piece=piece)
    wide_pack = call_kernel(
        pick,
        jax.ShapeDtypeStruct((model_part, 2 * hidden_here), bf16),
        smem_first=True,
        count=3,
    )(me.astype(jnp.int32)[None], gate_weight, up_weight)
    wide_all = lax.all_gather(wide_pack, "fsdp", axis=0, tiled=True)
    down_all = lax.all_gather(
        lax.dynamic_slice_in_dim(down_weight, me * piece, piece, 0),
        "fsdp",
        axis=0,
        tiled=True,
    )

    tokens_all = true_order(token_parts)
    upstream = cotangent[0]
    tokens_all, late_upstream = hold((tokens_all, upstream))
    upstream_parts = gather_ctx(late_upstream)
    upstream_all = jnp.concatenate(upstream_parts, axis=0)
    tokens_all = tokens_all.astype(f32)
    places = true_order(place_parts)
    normal_all, _ = unit_norm(tokens_all)
    normed = (normal_all * gain_one).astype(bf16)
    qkv = dot_plain(normed, qkv_weight)
    half_dim = HD // 2
    freqs = theta_base ** (-(jnp.arange(half_dim, dtype=f32) * 2.0) / HD)
    angles = places.astype(f32)[:, None] * jnp.tile(freqs, 4)[None, :]
    cosine = jnp.cos(angles)
    sine = jnp.sin(angles)
    q_heads = q_width // HD
    kv_heads = kv_width // HD
    block = 256
    sizes = dict(q_width=q_width, kv_width=kv_width, rows=rows, block=block)
    mixed_heads, q_low, k_low, v_low = call_kernel(
        functools.partial(attention_forward_kernel, **sizes),
        (
            jax.ShapeDtypeStruct((rows, q_width), bf16),
            jax.ShapeDtypeStruct((q_heads, rows, HD), bf16),
            jax.ShapeDtypeStruct((kv_heads, rows, HD), bf16),
            jax.ShapeDtypeStruct((kv_heads, rows, HD), bf16),
        ),
        scratch=(pltpu.VMEM((q_heads, rows, HD), bf16),),
        count=5,
    )(qkv, cosine, sine, gain_query, gain_key)
    head_parts = [rows_of(mixed_heads, 0)] + [send(rows_of(mixed_heads, s), s) for s in others]
    stacked = by_rank(head_parts)
    mixed = jnp.concatenate([stacked[r] for r in range(ranks)], axis=1)
    middle = own_tokens.astype(f32) + dot_plain(mixed, out_full)

    normal_two, inverse_two = unit_norm(middle)
    normed_two = (normal_two * gain_two).astype(bf16)
    normed_two_all = jnp.concatenate(gather_ctx(normed_two), axis=0)
    gate_all = wide_all[:, :hidden_here]
    up_all = wide_all[:, hidden_here:]
    gate = dot_plain(normed_two_all, gate_all)
    up_values = dot_plain(normed_two_all, up_all)
    sigma = jax.nn.sigmoid(gate)
    swish = gate * sigma
    act = (swish * up_values).astype(bf16)
    down_local = transposed_times(act, upstream_all).astype(bf16)
    down_all, down_local = hold((down_all, down_local))
    down_share = lax.psum_scatter(down_local, "fsdp", scatter_dimension=0, tiled=True)
    act_grad = times_transposed(upstream_all, down_all)
    gate_grad = (act_grad * up_values * sigma * (1.0 + gate * (1.0 - sigma))).astype(bf16)
    up_grad = (act_grad * swish).astype(bf16)

    def part_rows(value, step):
        return value[step * rows_here : (step + 1) * rows_here]

    def wide_back(step):
        return times_transposed(part_rows(gate_grad, step), gate_all) + times_transposed(
            part_rows(up_grad, step), up_all
        )

    back_parts = [send(wide_back(s).astype(bf16), s) for s in others]
    normed_two_grad = wide_back(0)
    wide_local = jnp.concatenate(
        [
            transposed_times(normed_two_all, gate_grad).astype(bf16),
            transposed_times(normed_two_all, up_grad).astype(bf16),
        ],
        axis=1,
    )
    out_partial = dot_plain(act, down_all).astype(bf16)
    back_parts, wide_local, out_partial = hold((back_parts, wide_local, out_partial))
    wide_share = lax.psum_scatter(wide_local, "fsdp", scatter_dimension=0, tiled=True)
    for part in back_parts:
        normed_two_grad = normed_two_grad + part.astype(f32)
    out_parts = [send(part_rows(out_partial, s), s) for s in others]
    middle_grad = upstream.astype(f32) + norm_backward(
        normed_two_grad * gain_two, normal_two, inverse_two
    )
    gain_two_grad = jnp.sum(normed_two_grad * normal_two, axis=0)

    middle_low = middle_grad.astype(bf16)
    mixed_grad = times_transposed(middle_low, out_full).astype(bf16)
    out_local = transposed_times(mixed, middle_low).astype(bf16)
    mixed_grad_parts = []
    for step in range(ranks):
        piece_of = lax.dynamic_slice_in_dim(mixed_grad, (me ^ step) * q_width, q_width, 1)
        mixed_grad_parts.append(send(piece_of, step) if step else piece_of)
    mixed_grad_parts, out_local = hold((mixed_grad_parts, out_local))
    out_share = lax.psum_scatter(out_local, "fsdp", scatter_dimension=0, tiled=True)
    mixed_grad_heads = true_order(mixed_grad_parts)
    qkv_grad, head_gain_grads = call_kernel(
        functools.partial(attention_backward_kernel, **sizes),
        (
            jax.ShapeDtypeStruct((rows, width), bf16),
            jax.ShapeDtypeStruct((8, 2 * HD), f32),
        ),
        scratch=(
            pltpu.VMEM((q_heads, rows, HD), bf16),
            pltpu.VMEM((q_heads, rows, HD), f32),
            pltpu.VMEM((kv_heads, rows, HD), f32),
            pltpu.VMEM((kv_heads, rows, HD), f32),
        ),
        count=9,
    )(qkv, cosine, sine, gain_query, gain_key, q_low, k_low, v_low, mixed_grad_heads)
    out_parts, late_middle, own_partial, _ = hold(
        (out_parts, middle, part_rows(out_partial, 0), qkv_grad)
    )
    result = late_middle + own_partial.astype(f32)
    for part in out_parts:
        result = result + part.astype(f32)
    result = result.astype(bf16)
    normed_grad = times_transposed(qkv_grad, qkv_weight)
    gain_one_grad = jnp.sum(normed_grad * normal_all, axis=0)
    normed_grad_low = normed_grad.astype(bf16)
    own_grad = rows_of(normed_grad_low, 0).astype(f32)
    own_parts = [send(rows_of(normed_grad_low, step), step) for step in others]
    for part in own_parts:
        own_grad = own_grad + part.astype(f32)
    normal_own, inverse_own = unit_norm(own_tokens.astype(f32))
    input_grad = (
        middle_grad + norm_backward(own_grad * gain_one, normal_own, inverse_own)
    ).astype(bf16)

    head_gains = head_gain_grads[:2, :HD] + head_gain_grads[:2, HD:]

    def gain_rows(grad, size):
        return jnp.pad(grad.reshape(owners, size), ((0, 0), (0, width - size)))

    gain_block = jnp.stack(
        [
            gain_rows(gain_one_grad, model_part),
            gain_rows(gain_two_grad, model_part),
            gain_rows(head_gains[0], head_part),
            gain_rows(head_gains[1], head_part),
        ],
        axis=1,
    )
    gain_block = hold(jnp.pad(gain_block.astype(bf16), ((0, 0), (0, 12), (0, 0))))
    weight_block = transposed_times(normed, qkv_grad).astype(bf16)
    grad_pack = jnp.concatenate(
        [weight_block.reshape(owners, model_part, width), gain_block], axis=1
    )
    attn_share = scatter_owners(grad_pack.reshape(chips, 2, model_part + 16, width))

    down_stack = by_rank(gather_ctx(down_share))
    grad_down = down_stack.reshape(ranks * piece, model).astype(f32)
    wide_stack = by_rank(gather_ctx(wide_share))
    spread = functools.partial(spread_kernel, shards_of=owners, ranks=ranks, piece=piece)
    grad_gate, grad_up = call_kernel(
        spread,
        (
            jax.ShapeDtypeStruct((model_part, hidden_width), f32),
            jax.ShapeDtypeStruct((model_part, hidden_width), f32),
        ),
        count=1,
    )(wide_stack)
    grad_out = sum(part.astype(f32) for part in gather_ctx(out_share))
    attn_stack = by_rank(gather_ctx(attn_share))

    def join(start, size):
        return jnp.concatenate(
            [attn_stack[r, :model_part, start : start + size] for r in range(ranks)], axis=1
        ).astype(f32)

    gain_sums = jnp.sum(attn_stack[:, model_part : model_part + 4].astype(f32), axis=0)
    return (
        result[None],
        input_grad[None],
        gain_sums[0, :model_part],
        gain_sums[2, :head_part],
        gain_sums[3, :head_part],
        join(0, q_width),
        join(q_width, kv_width),
        join(q_width + kv_width, kv_width),
        grad_out,
        gain_sums[1, :model_part],
        grad_gate,
        grad_up,
        grad_down,
    )


def solution(mesh):
    return jax.shard_map(
        shards,
        mesh=mesh,
        in_specs=(
            P("fsdp", "ctx", None),
            P("fsdp", "ctx"),
            P(),
            P("fsdp"),
            P("fsdp"),
            P("fsdp"),
            P("fsdp", None),
            P("fsdp", None),
            P("fsdp", None),
            P("fsdp", None),
            P("fsdp"),
            P("fsdp", None),
            P("fsdp", None),
            P("fsdp", None),
            P("fsdp", "ctx", None),
        ),
        out_specs=(
            P("fsdp", "ctx", None),
            P("fsdp", "ctx", None),
            P("fsdp"),
            P("fsdp"),
            P("fsdp"),
            P("fsdp", None),
            P("fsdp", None),
            P("fsdp", None),
            P("fsdp", None),
            P("fsdp"),
            P("fsdp", None),
            P("fsdp", None),
            P("fsdp", None),
        ),
        check_vma=False,
    )
```

```python
import functools

import jax
import jax.numpy as jnp
from jax import lax
from jax.experimental import pallas as pl
from jax.experimental.pallas import tpu as pltpu
from jax.sharding import PartitionSpec as P


H = 16
HD = 64
KV = 8
GROUPS = H // KV

epsilon = 1e-05
theta_base = 1000000.0
score_scale = 0.125
masked_value = -1e30


def dot_plain(left, right):
    return jnp.dot(left, right, preferred_element_type=jnp.float32)


def times_transposed(left, right):
    return lax.dot_general(
        left, right, (((1,), (1,)), ((), ())), preferred_element_type=jnp.float32
    )


def transposed_times(left, right):
    return lax.dot_general(
        left, right, (((0,), (0,)), ((), ())), preferred_element_type=jnp.float32
    )


def exact_dot(left, right):
    return jnp.dot(
        left, right, preferred_element_type=jnp.float32, precision=lax.Precision.HIGHEST
    )


def unit_norm(values):
    inverse = lax.rsqrt(jnp.mean(values * values, axis=-1, keepdims=True) + epsilon)
    return values * inverse, inverse


def norm_backward(scaled, normal, inverse):
    inner = jnp.mean(scaled * normal, axis=-1, keepdims=True)
    return inverse * (scaled - normal * inner)


def lane_tables(width):
    row = lax.broadcasted_iota(jnp.int32, (width, width), 0)
    col = lax.broadcasted_iota(jnp.int32, (width, width), 1)
    mean = jnp.where(row // HD == col // HD, 1.0 / HD, 0.0).astype(jnp.float32)
    low = col % HD < HD // 2
    partner = jnp.where(low, col + HD // 2, col - HD // 2)
    swap = jnp.where(row == partner, 1.0, 0.0).astype(jnp.float32)
    lane = lax.broadcasted_iota(jnp.int32, (1, width), 1)
    sign = jnp.where(lane % HD < HD // 2, -1.0, 1.0).astype(jnp.float32)
    return mean, swap, sign


def chunk_widths(width):
    step = min(width, 2 * HD)
    return [(start, step) for start in range(0, width, step)]


def attention_forward_kernel(
    qkv_ref, cos_ref, sin_ref, gq_ref, gk_ref, ob_ref, qs_ref, ks_ref, vs_ref, os_ref,
    *, q_width, kv_width, rows, block
):
    q_heads = q_width // HD
    kv_heads = kv_width // HD
    for base, width, gain_ref, out_ref, scale in (
        (0, q_width, gq_ref, qs_ref, score_scale),
        (q_width, kv_width, gk_ref, ks_ref, 1.0),
    ):
        for start, step in chunk_widths(width):
            mean, swap, sign = lane_tables(step)
            for row in range(0, rows, block):
                here = pl.ds(row, block)
                raw = qkv_ref[here, pl.ds(base + start, step)]
                inverse = lax.rsqrt(exact_dot(raw * raw, mean) + epsilon)
                normed = raw * inverse * gain_ref[:, :step]
                turned = normed * cos_ref[here, :step] + exact_dot(normed, swap) * (
                    sin_ref[here, :step] * sign
                )
                low = turned.astype(jnp.bfloat16) * jnp.bfloat16(scale)
                for part in range(step // HD):
                    out_ref[start // HD + part, here, :] = low[:, part * HD : (part + 1) * HD]
    for head in range(kv_heads):
        at = q_width + kv_width + head * HD
        vs_ref[head] = qkv_ref[:, pl.ds(at, HD)].astype(jnp.bfloat16)

    def one_head(head, carry):
        pair = head // GROUPS
        for row in range(0, rows, block):
            upto = row + block
            q_here = qs_ref[head, pl.ds(row, block), :]
            scores = times_transposed(q_here, ks_ref[pair, pl.ds(0, upto), :])
            own = lax.broadcasted_iota(jnp.int32, (block, upto), 0) + row
            other = lax.broadcasted_iota(jnp.int32, (block, upto), 1)
            scores = jnp.where(own >= other, scores, masked_value)
            top = jnp.max(scores, axis=-1, keepdims=True)
            expo = jnp.exp(scores - top)
            probs = (expo * (1.0 / jnp.sum(expo, axis=-1, keepdims=True))).astype(jnp.bfloat16)
            mixed = dot_plain(probs, vs_ref[pair, pl.ds(0, upto), :])
            os_ref[head, pl.ds(row, block), :] = mixed.astype(jnp.bfloat16)
        return carry

    lax.fori_loop(0, q_heads, one_head, 0)
    for head in range(q_heads):
        ob_ref[:, head * HD : (head + 1) * HD] = os_ref[head]


def attention_backward_kernel(
    qkv_ref, cos_ref, sin_ref, gq_ref, gk_ref, qs_ref, ks_ref, vs_ref, dob_ref,
    dqkv_ref, gains_ref, do_ref, dq_ref, dk_ref, dv_ref,
    *, q_width, kv_width, rows, block
):
    q_heads = q_width // HD
    kv_heads = kv_width // HD
    for head in range(q_heads):
        do_ref[head] = dob_ref[:, head * HD : (head + 1) * HD]
    dk_ref[...] = jnp.zeros_like(dk_ref)
    dv_ref[...] = jnp.zeros_like(dv_ref)

    def one_head(head, carry):
        pair = head // GROUPS
        for row in range(0, rows, block):
            upto = row + block
            here = pl.ds(row, block)
            seen = pl.ds(0, upto)
            q_here = qs_ref[head, here, :]
            do_here = do_ref[head, here, :]
            scores = times_transposed(q_here, ks_ref[pair, seen, :])
            own = lax.broadcasted_iota(jnp.int32, (block, upto), 0) + row
            other = lax.broadcasted_iota(jnp.int32, (block, upto), 1)
            scores = jnp.where(own >= other, scores, masked_value)
            top = jnp.max(scores, axis=-1, keepdims=True)
            expo = jnp.exp(scores - top)
            probs = expo * (1.0 / jnp.sum(expo, axis=-1, keepdims=True))
            prob_grad = times_transposed(do_here, vs_ref[pair, seen, :])
            inner = jnp.sum(probs * prob_grad, axis=-1, keepdims=True)
            score_grad = (probs * (prob_grad - inner)).astype(jnp.bfloat16)
            dq_ref[head, here, :] = dot_plain(score_grad, ks_ref[pair, seen, :]) * score_scale
            dk_ref[pair, seen, :] += transposed_times(score_grad, q_here)
            dv_ref[pair, seen, :] += transposed_times(probs.astype(jnp.bfloat16), do_here)
        return carry

    lax.fori_loop(0, q_heads, one_head, 0)
    gains_ref[...] = jnp.zeros_like(gains_ref)
    for slot, base, width, gain_ref, grad_ref in (
        (0, 0, q_width, gq_ref, dq_ref),
        (1, q_width, kv_width, gk_ref, dk_ref),
    ):
        for start, step in chunk_widths(width):
            mean, swap, sign = lane_tables(step)
            for row in range(0, rows, block):
                here = pl.ds(row, block)
                first = start // HD
                turned = jnp.concatenate(
                    [grad_ref[first + part, here, :] for part in range(step // HD)], axis=1
                )
                normed_grad = turned * cos_ref[here, :step] - exact_dot(turned, swap) * (
                    sin_ref[here, :step] * sign
                )
                raw = qkv_ref[here, pl.ds(base + start, step)]
                inverse = lax.rsqrt(exact_dot(raw * raw, mean) + epsilon)
                unit = raw * inverse
                gains_ref[slot : slot + 1, :step] += jnp.sum(
                    normed_grad * unit, axis=0, keepdims=True
                )
                scaled = normed_grad * gain_ref[:, :step]
                raw_grad = inverse * (scaled - unit * exact_dot(scaled * unit, mean))
                dqkv_ref[here, pl.ds(base + start, step)] = raw_grad.astype(jnp.bfloat16)
    for head in range(kv_heads):
        at = q_width + kv_width + head * HD
        dqkv_ref[:, at : at + HD] = dv_ref[head].astype(jnp.bfloat16)


def spread_kernel(parts_ref, gate_ref, up_ref, *, shards_of, ranks, piece):
    half = shards_of * piece
    for base, out_ref in ((0, gate_ref), (half, up_ref)):
        out_ref[...] = jnp.concatenate(
            [
                parts_ref[rank, :, base + shard * piece : base + (shard + 1) * piece]
                for shard in range(shards_of)
                for rank in range(ranks)
            ],
            axis=1,
        ).astype(jnp.float32)


def pick_kernel(rank_ref, gate_ref, up_ref, out_ref, *, shards_of, ranks, piece):
    half = shards_of * piece
    for rank in range(ranks):

        @pl.when(rank_ref[0] == rank)
        def _():
            for base, in_ref in ((0, gate_ref), (half, up_ref)):
                out_ref[:, base : base + half] = jnp.concatenate(
                    [
                        in_ref[:, (shard * ranks + rank) * piece : (shard * ranks + rank + 1) * piece]
                        for shard in range(shards_of)
                    ],
                    axis=1,
                )


def place_kernel(starts_ref, *refs, half):
    out_ref = refs[-1]
    for number, part_ref in enumerate(refs[:-1]):
        for side in range(2):
            start = pl.multiple_of(starts_ref[2 * number + side], 64)
            out_ref[pl.ds(start, half), :] = part_ref[side * half : (side + 1) * half, :]


def call_kernel(kernel, out_shapes, scratch=(), smem_first=False, count=0):
    vmem = pl.BlockSpec(memory_space=pltpu.VMEM)
    in_specs = [vmem] * count
    if smem_first:
        in_specs[0] = pl.BlockSpec(memory_space=pltpu.SMEM)
    return pl.pallas_call(
        kernel,
        out_shape=out_shapes,
        in_specs=in_specs,
        out_specs=jax.tree.map(lambda _: vmem, out_shapes),
        scratch_shapes=scratch,
        compiler_params=pltpu.CompilerParams(vmem_limit_bytes=56 * 1024 * 1024),
    )


def shards(
    tokens,
    positions,
    block_pairs,
    input_gain,
    query_gain,
    key_gain,
    query_weight,
    key_weight,
    value_weight,
    out_weight,
    middle_gain,
    gate_weight,
    up_weight,
    down_weight,
    cotangent,
):
    ranks = lax.axis_size("ctx")
    owners = lax.axis_size("fsdp")
    me = lax.axis_index("ctx")
    own_tokens = tokens[0]
    rows_here, model = own_tokens.shape
    half_rows = rows_here // 2
    rows = rows_here * ranks
    others = range(1, ranks)
    bf16 = jnp.bfloat16
    f32 = jnp.float32
    q_width = H // ranks * HD
    kv_width = KV // ranks * HD
    width = q_width + 2 * kv_width
    model_part = model // owners
    hidden_width = gate_weight.shape[1]
    piece = hidden_width // (owners * ranks)
    hidden_here = owners * piece

    def send(value, step):
        return lax.ppermute(value, "ctx", [(i, i ^ step) for i in range(ranks)])

    def gather_ctx(value):
        return [value] + [send(value, step) for step in others]

    def by_rank(parts):
        stack = jnp.zeros((ranks,) + parts[0].shape, parts[0].dtype)
        for step, part in enumerate(parts):
            stack = lax.dynamic_update_index_in_dim(stack, part, me ^ step, 0)
        return stack

    place = lax.axis_index("fsdp")
    core = place % 2
    chip = place // 2
    chips = owners // 2

    def send_owner(value, step):
        return lax.ppermute(value, "fsdp", [(i, i ^ step) for i in range(owners)])

    def gather_owners(value):
        stack = jnp.zeros((chips,) + value.shape, value.dtype)
        for step in range(chips):
            part = send_owner(value, 2 * step) if step else value
            stack = lax.dynamic_update_index_in_dim(stack, part, chip ^ step, 0)
        partner = send_owner(stack, 1)
        first = jnp.where(core == 0, stack, partner)
        second = jnp.where(core == 0, partner, stack)
        return jnp.stack([first, second], axis=1)

    def scatter_owners(value):
        mine = jnp.where(core == 0, value[:, 0], value[:, 1])
        theirs = send_owner(jnp.where(core == 0, value[:, 1], value[:, 0]), 1)
        pair = (mine.astype(f32) + theirs.astype(f32)).astype(bf16)
        total = lax.dynamic_index_in_dim(pair, chip, 0, keepdims=False).astype(f32)
        for step in range(1, chips):
            entry = lax.dynamic_index_in_dim(pair, chip ^ step, 0, keepdims=False)
            total = total + send_owner(entry, 2 * step).astype(f32)
        return total.astype(bf16)

    hold = lax.optimization_barrier

    def block_starts(step):
        low = lax.dynamic_index_in_dim(block_pairs, me ^ step, 0, keepdims=False)
        return low * half_rows, (2 * ranks - 1 - low) * half_rows

    def true_order(parts):
        out = jnp.zeros((rows,) + parts[0].shape[1:], parts[0].dtype)
        for step, part in enumerate(parts):
            low, high = block_starts(step)
            out = lax.dynamic_update_slice_in_dim(out, part[:half_rows], low, 0)
            out = lax.dynamic_update_slice_in_dim(out, part[half_rows:], high, 0)
        return out

    all_ranks = jnp.arange(ranks, dtype=jnp.int32)
    low_blocks = jnp.sum(
        jnp.where((all_ranks ^ me)[:, None] == all_ranks[None, :], block_pairs[None, :], 0), axis=1
    )
    starts = jnp.stack([low_blocks, 2 * ranks - 1 - low_blocks], axis=1).reshape(-1) * half_rows

    def placed(parts):
        return call_kernel(
            functools.partial(place_kernel, half=half_rows),
            jax.ShapeDtypeStruct((rows, parts[0].shape[1]), parts[0].dtype),
            smem_first=True,
            count=1 + ranks,
        )(starts.astype(jnp.int32), *parts)

    def rows_of(value, step):
        low, high = block_starts(step)
        return jnp.concatenate(
            [
                lax.dynamic_slice_in_dim(value, low, half_rows, 0),
                lax.dynamic_slice_in_dim(value, high, half_rows, 0),
            ],
            axis=0,
        )

    def columns(weight, size):
        return lax.dynamic_slice_in_dim(weight, me * size, size, 1)

    def gain_row(gain):
        return jnp.pad(gain, (0, width - gain.shape[0]))[None]

    attn_pack = jnp.concatenate(
        [
            columns(query_weight, q_width),
            columns(key_weight, kv_width),
            columns(value_weight, kv_width),
        ],
        axis=1,
    )
    gain_pack = jnp.concatenate(
        [gain_row(g) for g in (input_gain, middle_gain, query_gain, key_gain)]
        + [jnp.zeros((12, width), bf16)],
        axis=0,
    )
    token_parts = gather_ctx(own_tokens)
    place_parts = gather_ctx(positions[0])
    attn_all = gather_owners(
        jnp.concatenate([attn_pack, gain_pack], axis=0)
    ).reshape(owners, model_part + 16, width)
    qkv_weight = attn_all[:, :model_part].reshape(model, width)
    gain_one = attn_all[:, model_part, :model_part].reshape(1, model).astype(f32)
    gain_two = attn_all[:, model_part + 1, :model_part].reshape(1, model).astype(f32)
    head_part = HD // owners
    gain_query = attn_all[:, model_part + 2, :head_part].reshape(1, HD).astype(f32)
    gain_key = attn_all[:, model_part + 3, :head_part].reshape(1, HD).astype(f32)
    gain_query = jnp.tile(gain_query, (1, 2))
    gain_key = jnp.tile(gain_key, (1, 2))
    out_full = lax.all_gather(out_weight, "fsdp", axis=0, tiled=True)
    pick = functools.partial(pick_kernel, shards_of=owners, ranks=ranks, piece=piece)
    wide_pack = call_kernel(
        pick,
        jax.ShapeDtypeStruct((model_part, 2 * hidden_here), bf16),
        smem_first=True,
        count=3,
    )(me.astype(jnp.int32)[None], gate_weight, up_weight)
    wide_all = lax.all_gather(wide_pack, "fsdp", axis=0, tiled=True)
    down_all = lax.all_gather(
        lax.dynamic_slice_in_dim(down_weight, me * piece, piece, 0),
        "fsdp",
        axis=0,
        tiled=True,
    )

    tokens_all = placed(token_parts)
    upstream = cotangent[0]
    tokens_all, late_upstream = hold((tokens_all, upstream))
    upstream_parts = gather_ctx(late_upstream)
    upstream_all = jnp.concatenate(upstream_parts, axis=0)
    tokens_all = tokens_all.astype(f32)
    places = true_order(place_parts)
    normal_all, _ = unit_norm(tokens_all)
    normed = (normal_all * gain_one).astype(bf16)
    qkv = dot_plain(normed, qkv_weight)
    half_dim = HD // 2
    freqs = theta_base ** (-(jnp.arange(half_dim, dtype=f32) * 2.0) / HD)
    angles = places.astype(f32)[:, None] * jnp.tile(freqs, 4)[None, :]
    cosine = jnp.cos(angles)
    sine = jnp.sin(angles)
    q_heads = q_width // HD
    kv_heads = kv_width // HD
    block = 256
    sizes = dict(q_width=q_width, kv_width=kv_width, rows=rows, block=block)
    mixed_heads, q_low, k_low, v_low = call_kernel(
        functools.partial(attention_forward_kernel, **sizes),
        (
            jax.ShapeDtypeStruct((rows, q_width), bf16),
            jax.ShapeDtypeStruct((q_heads, rows, HD), bf16),
            jax.ShapeDtypeStruct((kv_heads, rows, HD), bf16),
            jax.ShapeDtypeStruct((kv_heads, rows, HD), bf16),
        ),
        scratch=(pltpu.VMEM((q_heads, rows, HD), bf16),),
        count=5,
    )(qkv, cosine, sine, gain_query, gain_key)
    head_parts = [rows_of(mixed_heads, 0)] + [send(rows_of(mixed_heads, s), s) for s in others]
    stacked = by_rank(head_parts)
    mixed = jnp.concatenate([stacked[r] for r in range(ranks)], axis=1)
    middle = own_tokens.astype(f32) + dot_plain(mixed, out_full)

    normal_two, inverse_two = unit_norm(middle)
    normed_two = (normal_two * gain_two).astype(bf16)
    normed_two_all = jnp.concatenate(gather_ctx(normed_two), axis=0)
    gate_all = wide_all[:, :hidden_here]
    up_all = wide_all[:, hidden_here:]
    gate = dot_plain(normed_two_all, gate_all)
    up_values = dot_plain(normed_two_all, up_all)
    sigma = jax.nn.sigmoid(gate)
    swish = gate * sigma
    act = (swish * up_values).astype(bf16)
    down_local = transposed_times(act, upstream_all).astype(bf16)
    down_all, down_local = hold((down_all, down_local))
    down_share = lax.psum_scatter(down_local, "fsdp", scatter_dimension=0, tiled=True)
    act_grad = times_transposed(upstream_all, down_all)
    gate_grad = (act_grad * up_values * sigma * (1.0 + gate * (1.0 - sigma))).astype(bf16)
    up_grad = (act_grad * swish).astype(bf16)

    def part_rows(value, step):
        return value[step * rows_here : (step + 1) * rows_here]

    def wide_back(step):
        return times_transposed(part_rows(gate_grad, step), gate_all) + times_transposed(
            part_rows(up_grad, step), up_all
        )

    back_parts = [send(wide_back(s).astype(bf16), s) for s in others]
    normed_two_grad = wide_back(0)
    wide_local = jnp.concatenate(
        [
            transposed_times(normed_two_all, gate_grad).astype(bf16),
            transposed_times(normed_two_all, up_grad).astype(bf16),
        ],
        axis=1,
    )
    late_act, _ = hold((act, gate_grad))
    out_partial = dot_plain(late_act, down_all).astype(bf16)
    back_parts, normed_two_grad, wide_local, out_partial = hold(
        (back_parts, normed_two_grad, wide_local, out_partial)
    )
    wide_share = lax.psum_scatter(wide_local, "fsdp", scatter_dimension=0, tiled=True)
    for part in back_parts:
        normed_two_grad = normed_two_grad + part.astype(f32)
    out_parts = [send(part_rows(out_partial, s), s) for s in others]
    middle_grad = upstream.astype(f32) + norm_backward(
        normed_two_grad * gain_two, normal_two, inverse_two
    )
    gain_two_grad = jnp.sum(normed_two_grad * normal_two, axis=0)

    middle_low = middle_grad.astype(bf16)
    mixed_grad = times_transposed(middle_low, out_full).astype(bf16)
    out_local = transposed_times(mixed, middle_low).astype(bf16)
    mixed_grad_parts = []
    for step in range(ranks):
        piece_of = lax.dynamic_slice_in_dim(mixed_grad, (me ^ step) * q_width, q_width, 1)
        mixed_grad_parts.append(send(piece_of, step) if step else piece_of)
    mixed_grad_parts, out_local = hold((mixed_grad_parts, out_local))
    out_share = lax.psum_scatter(out_local, "fsdp", scatter_dimension=0, tiled=True)
    mixed_grad_heads = placed(mixed_grad_parts)
    qkv_grad, head_gain_grads = call_kernel(
        functools.partial(attention_backward_kernel, **sizes),
        (
            jax.ShapeDtypeStruct((rows, width), bf16),
            jax.ShapeDtypeStruct((8, 2 * HD), f32),
        ),
        scratch=(
            pltpu.VMEM((q_heads, rows, HD), bf16),
            pltpu.VMEM((q_heads, rows, HD), f32),
            pltpu.VMEM((kv_heads, rows, HD), f32),
            pltpu.VMEM((kv_heads, rows, HD), f32),
        ),
        count=9,
    )(qkv, cosine, sine, gain_query, gain_key, q_low, k_low, v_low, mixed_grad_heads)
    out_parts, late_middle, own_partial, _ = hold(
        (out_parts, middle, part_rows(out_partial, 0), qkv_grad)
    )
    result = late_middle + own_partial.astype(f32)
    for part in out_parts:
        result = result + part.astype(f32)
    result = result.astype(bf16)
    weight_block = transposed_times(normed, qkv_grad).astype(bf16)
    weight_block, qkv_grad = hold((weight_block, qkv_grad))
    normed_grad = times_transposed(qkv_grad, qkv_weight)
    gain_one_grad = jnp.sum(normed_grad * normal_all, axis=0)
    normed_grad_low = normed_grad.astype(bf16)
    own_grad = rows_of(normed_grad_low, 0).astype(f32)
    own_parts = [send(rows_of(normed_grad_low, step), step) for step in others]
    for part in own_parts:
        own_grad = own_grad + part.astype(f32)
    normal_own, inverse_own = unit_norm(own_tokens.astype(f32))
    input_grad = (
        middle_grad + norm_backward(own_grad * gain_one, normal_own, inverse_own)
    ).astype(bf16)

    head_gains = head_gain_grads[:2, :HD] + head_gain_grads[:2, HD:]

    def gain_rows(grad, size):
        return jnp.pad(grad.reshape(owners, size), ((0, 0), (0, width - size)))

    gain_block = jnp.stack(
        [
            gain_rows(gain_one_grad, model_part),
            gain_rows(gain_two_grad, model_part),
            gain_rows(head_gains[0], head_part),
            gain_rows(head_gains[1], head_part),
        ],
        axis=1,
    )
    gain_block = hold(jnp.pad(gain_block.astype(bf16), ((0, 0), (0, 12), (0, 0))))
    grad_pack = jnp.concatenate(
        [weight_block.reshape(owners, model_part, width), gain_block], axis=1
    )
    attn_share = scatter_owners(grad_pack.reshape(chips, 2, model_part + 16, width))

    down_stack = by_rank(gather_ctx(down_share))
    grad_down = down_stack.reshape(ranks * piece, model).astype(f32)
    wide_stack = by_rank(gather_ctx(wide_share))
    spread = functools.partial(spread_kernel, shards_of=owners, ranks=ranks, piece=piece)
    grad_gate, grad_up = call_kernel(
        spread,
        (
            jax.ShapeDtypeStruct((model_part, hidden_width), f32),
            jax.ShapeDtypeStruct((model_part, hidden_width), f32),
        ),
        count=1,
    )(wide_stack)
    grad_out = sum(part.astype(f32) for part in gather_ctx(out_share))
    attn_stack = by_rank(gather_ctx(attn_share))

    def join(start, size):
        return jnp.concatenate(
            [attn_stack[r, :model_part, start : start + size] for r in range(ranks)], axis=1
        ).astype(f32)

    gain_sums = jnp.sum(attn_stack[:, model_part : model_part + 4].astype(f32), axis=0)
    return (
        result[None],
        input_grad[None],
        gain_sums[0, :model_part],
        gain_sums[2, :head_part],
        gain_sums[3, :head_part],
        join(0, q_width),
        join(q_width, kv_width),
        join(q_width + kv_width, kv_width),
        grad_out,
        gain_sums[1, :model_part],
        grad_gate,
        grad_up,
        grad_down,
    )


def solution(mesh):
    return jax.shard_map(
        shards,
        mesh=mesh,
        in_specs=(
            P("fsdp", "ctx", None),
            P("fsdp", "ctx"),
            P(),
            P("fsdp"),
            P("fsdp"),
            P("fsdp"),
            P("fsdp", None),
            P("fsdp", None),
            P("fsdp", None),
            P("fsdp", None),
            P("fsdp"),
            P("fsdp", None),
            P("fsdp", None),
            P("fsdp", None),
            P("fsdp", "ctx", None),
        ),
        out_specs=(
            P("fsdp", "ctx", None),
            P("fsdp", "ctx", None),
            P("fsdp"),
            P("fsdp"),
            P("fsdp"),
            P("fsdp", None),
            P("fsdp", None),
            P("fsdp", None),
            P("fsdp", None),
            P("fsdp"),
            P("fsdp", None),
            P("fsdp", None),
            P("fsdp", None),
        ),
        check_vma=False,
    )
```
